256 devices in a mesh: space: 64 (over x, z, core), chan: 4 (over y).
Axes of the slice: x: 4, y: 4, z: 8, core: 2. Of those that a mesh axis runs over, the one named last changes fastest.
Arguments:
- features: bfloat16 [8192, 512], P('space', 'chan'), may hold values from -6 to 6
- mask: int32 [8192], P('space'), may hold values 0 or 1
- rulebook: int32 [128, 27], P('space'), may hold values from -1 to 127, as said below
- weight_first: bfloat16 [512, 27, 512], P('space', None, 'chan'), may hold values from -0.0546875 to 0.0546875
- weight_second: bfloat16 [512, 27, 512], P('space', None, 'chan'), may hold values from -0.0546875 to 0.0546875
- cotangent: bfloat16 [8192, 512], P('space', 'chan'), may hold values from -6 to 6
Outputs:
- output: bfloat16 [8192, 512], P('space', 'chan')
- features_grad: bfloat16 [8192, 512], P('space', 'chan')
- weight_first_grad: float32 [512, 27, 512], P('space', None, 'chan')
- weight_second_grad: float32 [512, 27, 512], P('space', None, 'chan')
The draws below stay inside these ranges and needn't reach their ends.
Inputs may be any that keep to these rules, and one draw needn't show every extreme that they name: `rulebook`: entry [b, c] is the brick that feeds brick b through brick offset c, or -1 for none; entry 13 is b itself. A brick of another device belongs to a device s one or two indices away; if it feeds the device s + 1, s + 2, s - 1 or s - 2 (k = 0, 1, 2, 3 respectively), it is brick s * 2 + ((k + h) mod 2) for some h below 1.
All inputs are finite; a program needn't handle non-finite values. No bound on the sum of `mask` on one device may be relied on, other than what follows from the above.
Results may differ from the reference program's by a relative error of at most 0.005.
Values may be sent and summed in bfloat16 or wider, within the bound.
No kernel may reach another device: no remote copies, remote signals or barrier semaphores. Data moves between devices by JAX's collectives and lax.ppermute only.
A program may use at most 128 MiB of HBM per device.

```python
import jax
import jax.numpy as jnp
import numpy as np
from jax import lax

C = 512
OFFSETS = 27
BR_DEV = 2
HB = 1
BRICKS = 128
VOXELS = 8192
N_SPACE = 64


def draw_rulebook(key, part):
    base = jax.random.fold_in(key, 23)
    kinds = jax.random.randint(jax.random.fold_in(base, 1), (BRICKS, 27), 0, 10)
    slots = jax.random.randint(jax.random.fold_in(base, 2), (BRICKS, 27), 0, HB)
    locals_drawn = jax.random.randint(jax.random.fold_in(base, 3), (BRICKS, 27), 0, BR_DEV)
    device = (jnp.arange(BRICKS, dtype=jnp.int32) // BR_DEV)[:, None]
    steps = jnp.array([1, 2, -1, -2], jnp.int32)
    position = (kinds - 3) % 4
    source = device - steps[position]
    valid = (source >= 0) & (source < N_SPACE)
    clipped = jnp.clip(source, 0, N_SPACE - 1)
    remote = clipped * BR_DEV + (position * HB + slots) % BR_DEV
    local_brick = device * BR_DEV + locals_drawn
    is_remote = (kinds >= 3) & (kinds < 9) & valid
    chosen = jnp.where(kinds == 9, -1, jnp.where(is_remote, remote, local_brick))
    center = (jnp.arange(27) == 13)[None, :]
    itself = jnp.arange(BRICKS, dtype=jnp.int32)[:, None]
    return jnp.where(center, itself, chosen).astype(jnp.int32)


def touch_ends(result, stream_key, least, top_value):
    dims = result.shape
    spot = [jax.random.randint(jax.random.fold_in(stream_key, axis), (), 0, dims[axis]) for axis in range(len(dims))]
    result = result.at[tuple(spot)].set(least)
    longest = dims.index(max(dims))
    spot[longest] = (spot[longest] + 1) % dims[longest]
    return result.at[tuple(spot)].set(top_value)


def block_levels(stream_key, extent, split, smallest, top_value):
    loudness = 1.0
    for dim, parts in split:
        draws = jax.random.uniform(jax.random.fold_in(jax.random.fold_in(stream_key, 6), dim), (parts,), jnp.float32, smallest / len(split), top_value / len(split))
        loudness = loudness * jnp.repeat(jnp.exp(draws), extent[dim] // parts).reshape((-1,) + (1,) * (len(extent) - 1 - dim))
    return loudness


def scatter_about(stream_key, extent, scale, most, shards=(), kind=jnp.bfloat16):
    result = jax.random.normal(stream_key, extent, jnp.float32) * scale
    if len(shards) > 0:
        result = block_levels(stream_key, extent, shards, -0.22, 0.18) * result
    return jnp.clip(result, min=-most, max=most).astype(kind)


def setup_inputs(seed: int = 0) -> dict:
    key_list = jax.random.split(jax.random.key(seed), 7)
    features = scatter_about(key_list[0], (VOXELS, C), 1.0, 6.0, ((0, 64), (1, 4)))
    mask = touch_ends((jax.random.randint(key_list[1], (VOXELS,), 0, 4) < 3).astype(jnp.int32), jax.random.fold_in(key_list[1], 1), 0, 1)
    rulebook = draw_rulebook(jax.random.fold_in(key_list[6], 71), 0)
    weight_first = scatter_about(key_list[3], (C, OFFSETS, C), (OFFSETS * C) ** -0.5, 0.0546875, ((0, 64), (2, 4)))
    weight_second = scatter_about(key_list[4], (C, OFFSETS, C), (OFFSETS * C) ** -0.5, 0.0546875, ((0, 64), (2, 4)))
    cotangent = scatter_about(key_list[5], (VOXELS, C), 1.0, 6.0, ((0, 64), (1, 4)))
    return dict(features=features, mask=mask, rulebook=rulebook, weight_first=weight_first, weight_second=weight_second, cotangent=cotangent)


def offset_tables():
    brick_table = np.zeros((27, 64), np.int32)
    cell_table = np.zeros((27, 64), np.int32)
    for offset in range(27):
        moves = (offset // 9 - 1, offset // 3 % 3 - 1, offset % 3 - 1)
        for voxel in range(64):
            cells = (voxel // 16, voxel // 4 % 4, voxel % 4)
            target = [cells[axis_number] + moves[axis_number] for axis_number in range(3)]
            brick_table[offset, voxel] = (target[0] // 4 + 1) * 9 + (target[1] // 4 + 1) * 3 + (target[2] // 4 + 1)
            cell_table[offset, voxel] = target[0] % 4 * 16 + target[1] % 4 * 4 + target[2] % 4
    return (brick_table, cell_table)

def reference(features, mask, rulebook, weight_first, weight_second, cotangent):
    brick_table, cell_table = offset_tables()
    voxel_count = features.shape[0]
    active = mask.astype(jnp.float32)[:, None]
    nearby = rulebook[:, brick_table]
    lookup = jnp.where(nearby >= 0, nearby * 64 + cell_table[None], voxel_count)
    lookup = jnp.transpose(lookup, (1, 0, 2)).reshape(27, voxel_count).astype(jnp.int32)
    offsets = jnp.arange(27, dtype=jnp.int32)
    masked = (features.astype(jnp.float32) * active).astype(jnp.bfloat16)

    def padded_of(source):
        return jnp.concatenate([source, jnp.zeros((1, source.shape[1]), source.dtype)], 0)

    def convolve(source, weight):
        padded = padded_of(source)

        def advance(running, offset):
            picked = jnp.take(padded, lookup[offset], axis=0)
            kernel = lax.dynamic_index_in_dim(weight, offset, 1, keepdims=False)
            return (running + jnp.dot(picked, kernel, preferred_element_type=jnp.float32), None)
        running, unused = lax.scan(advance, jnp.zeros((voxel_count, weight.shape[2]), jnp.float32), offsets)
        return running

    def transposed(gradient, weight):

        def advance(running, offset):
            kernel = lax.dynamic_index_in_dim(weight, offset, 1, keepdims=False)
            contrib = lax.dot_general(gradient, kernel, (((1,), (1,)), ((), ())), preferred_element_type=jnp.float32)
            return (running.at[lookup[offset]].add(contrib), None)
        running, unused = lax.scan(advance, jnp.zeros((voxel_count + 1, weight.shape[0]), jnp.float32), offsets)
        return running[:voxel_count]

    def kernel_grad(source, gradient):
        padded = padded_of(source)

        def advance(carry, offset):
            picked = jnp.take(padded, lookup[offset], axis=0)
            return (carry, lax.dot_general(picked, gradient, (((0,), (0,)), ((), ())), preferred_element_type=jnp.float32))
        unused, stacked = lax.scan(advance, jnp.float32(0.0), offsets)
        return jnp.transpose(stacked, (1, 0, 2))
    first_act = active * convolve(masked, weight_first)
    hidden = jax.nn.silu(first_act).astype(jnp.bfloat16)
    second_act = active * convolve(hidden, weight_second)
    output = second_act.astype(jnp.bfloat16)
    grad_second = (cotangent.astype(jnp.float32) * active).astype(jnp.bfloat16)
    weight_second_grad = kernel_grad(hidden, grad_second)
    hidden_grad = transposed(grad_second, weight_second)
    sigmoid_first = jax.nn.sigmoid(first_act)
    grad_first = (active * hidden_grad * sigmoid_first * (1.0 + first_act * (1.0 - sigmoid_first))).astype(jnp.bfloat16)
    weight_first_grad = kernel_grad(masked, grad_first)
    features_grad = (active * transposed(grad_first, weight_first)).astype(jnp.bfloat16)
    return (output, features_grad, weight_first_grad, weight_second_grad)
```

```python
import jax
import jax.numpy as jnp
import numpy as np
from jax import lax
from jax.experimental import pallas as pl
from jax.experimental.pallas import tpu as pltpu
from jax.sharding import Mesh
from jax.sharding import PartitionSpec as P

STEPS = (1, 2, -1, -2)
SPACE = ("x", "z", "core")
CELLS = 224
BF = jnp.bfloat16
F32 = jnp.float32


def tables():
    pick = np.zeros((CELLS, 32), np.float32)
    pick_back = np.zeros((CELLS, 32), np.float32)
    local = np.zeros((CELLS, 128), np.float32)
    for row in range(216):
        cell = (row // 36, row // 6 % 6, row % 6)
        side = [(v == 5) - (v == 0) for v in cell]
        at = [(v - 1) % 4 for v in cell]
        pick[row, 9 * (side[0] + 1) + 3 * (side[1] + 1) + side[2] + 1] = 1
        pick_back[row, 9 * (1 - side[0]) + 3 * (1 - side[1]) + 1 - side[2]] = 1
        voxel = at[0] * 16 + at[1] * 4 + at[2]
        local[row, voxel] = 1
        local[row, 64 + voxel] = 1
    spread = np.zeros((9, 6, 4, 4, CELLS), np.float32)
    for move in range(9):
        for i in range(6):
            for j in range(4):
                for k in range(4):
                    spread[move, i, j, k, i * 36 + (j + move // 3) * 6 + k + move % 3] = 1
    lanes = np.zeros((128, 2048), np.float32)
    for brick in range(2):
        for column in range(384):
            lanes[brick * 6 + column // 64, brick * 384 + column] = 1
        for column in range(640):
            lanes[12 + brick * 10 + column // 64, 768 + brick * 640 + column] = 1
    lane = np.arange(128)
    device = np.where((lane >= 12) & (lane < 32), (lane - 12) % 10 // 2, 0)
    sources = np.zeros((16, 128), np.float32)
    sources[device, lane] = 1
    as_bf = lambda value: jnp.asarray(value, BF)
    return (
        as_bf(pick),
        as_bf(pick_back),
        jnp.asarray(local),
        as_bf(spread.reshape(864, CELLS)),
        as_bf(lanes),
        as_bf(sources),
    )


def dot(a, b):
    return jnp.dot(a, b, preferred_element_type=F32)


def fill(out, base, matches, rows, pick, local, spread):
    count = rows.shape[0]
    padded = []
    for brick in range(2):
        chosen = dot(pick, matches[:, brick * count : (brick + 1) * count])
        select = (chosen * jnp.concatenate([local] * (count // 128), axis=1)).astype(BF)
        padded.append(dot(select, rows).astype(BF))
    wide = dot(spread, jnp.concatenate(padded, axis=1)).astype(BF)
    for brick in range(2):
        out[base + brick] = wide[:, brick * 128 : (brick + 1) * 128].reshape(9, 96, 128)


def block(ref, offset):
    start = offset // 9 * 16
    return ref[:, offset % 9, start : start + 64, :].reshape(512, 128)


def convolve(ref, weight):
    total = None
    for offset in range(27):
        part = dot(block(ref, offset), weight[offset])
        total = part if total is None else total + part
    return total


def convolve_back(ref, weight):
    total = None
    for offset in range(27):
        part = lax.dot_general(
            block(ref, 26 - offset), weight[offset], (((1,), (1,)), ((), ())), preferred_element_type=F32
        )
        total = part if total is None else total + part
    return total


def around(ids, own, before, after, other, turn):
    return (
        own.at[turn],
        other.at[1 - ids[2], (turn - ids[3] * (1 - ids[2])) & 3],
        before.at[(turn - ids[3]) & 3],
        other.at[ids[2], (turn + ids[4] * ids[2]) & 3],
        after.at[(turn + ids[4]) & 3],
    )


def gather_first(
    ids, mine, before, after, other, pick, pick_back, local, spread, lanes, sources, q_in, q_back, own, matched
):
    @pl.loop(0, 4)
    def _(turn):
        at = (ids[1] + turn) & 3
        views = around(ids, mine, before, after, other, turn)
        compact = None
        for device, view in enumerate(views):
            part = view[192:224, :] * sources[device : device + 1, :]
            compact = part if compact is None else compact + part
        matched[at] = compact
        own[at] = views[0][64:192, :]
        found = dot(compact, lanes[...]).astype(BF)
        rows = [views[0][0:64, :], views[0][224:288, :]]
        rows += [view[device % 2 * 224 : device % 2 * 224 + 64, :] for device, view in enumerate(views[1:])]
        fill(q_in, at * 2, found[:, :768], jnp.concatenate(rows, 0), pick[...], local[...], spread[...])
        rows = jnp.concatenate([view[64:192, :] for view in views], 0)
        fill(q_back, at * 2, found[:, 768:], rows, pick_back[...], local[...], spread[...])


def apply_first(q_in, q_back, weights, out):
    forward = convolve(q_in, weights.at[0])
    backward = convolve_back(q_back, weights.at[1])
    for at in range(4):
        out[at, 0:128, :] = forward[at * 128 : (at + 1) * 128]
        out[at, 128:256, :] = backward[at * 128 : (at + 1) * 128]


def weight_blocks(ref, gradient, keep, send, scratch, core):
    @pl.loop(0, 3)
    def _(move):
        start = pl.multiple_of(move * 16, 16)
        for rest in range(9):
            columns = ref[:, rest, pl.ds(start, 64), :].reshape(512, 128)
            scratch[rest % 2] = lax.dot_general(
                columns, gradient, (((0,), (0,)), ((), ())), preferred_element_type=F32
            )
            for z in range(8):
                keep[z, move * 9 + rest] = scratch[rest % 2, pl.ds(z * 16 + core * 8, 8), :]
                send[z, move * 9 + rest] = scratch[rest % 2, pl.ds(z * 16 + 8 - core * 8, 8), :]


def weigh_first(ids, mine, q_in, keep, send, own, scratch):
    for turn in range(4):
        own[(ids[0] + turn) & 3] = mine[turn, 128:256, :]
    weight_blocks(q_in, own[...].reshape(512, 128), keep, send, scratch, ids[2])


def apply_second(
    ids, mine, before, after, other, matched, own, weights, pick, pick_back, local, spread, lanes, sources,
    reduced, keep, send, q_hidden, q_back, scratch,
):
    @pl.loop(0, 4)
    def _(turn):
        at = (ids[0] + turn) & 3
        views = around(ids, mine, before, after, other, turn)
        found = dot(matched[at], lanes[...]).astype(BF)
        rows = [views[0][0:128, :]]
        rows += [view[device % 2 * 64 : device % 2 * 64 + 64, :] for device, view in enumerate(views[1:])]
        fill(q_hidden, at * 2, found[:, :768], jnp.concatenate(rows, 0), pick[...], local[...], spread[...])
        rows = jnp.concatenate([view[128:256, :] for view in views], 0)
        fill(q_back, at * 2, found[:, 768:], rows, pick_back[...], local[...], spread[...])

    forward = convolve(q_hidden, weights.at[1])
    backward = convolve_back(q_back, weights.at[0])
    for at in range(4):
        turn = (at - ids[1]) & 3
        reduced[turn, 0:128, :] = forward[at * 128 : (at + 1) * 128]
        reduced[turn, 128:256, :] = backward[at * 128 : (at + 1) * 128]
    weight_blocks(q_hidden, own[...].reshape(512, 128), keep, send, scratch, ids[2])


def call(kernel, outs, scratch, *args):
    smem = pl.BlockSpec(memory_space=pltpu.SMEM)
    vmem = pl.BlockSpec(memory_space=pltpu.VMEM)
    return pl.pallas_call(
        kernel,
        out_shape=outs,
        in_specs=[smem if value.dtype == jnp.int32 else vmem for value in args],
        out_specs=[vmem] * len(outs),
        scratch_shapes=scratch,
        compiler_params=pltpu.CompilerParams(vmem_limit_bytes=52 * 2**20),
    )(*args)


def spread_out(mine):
    before = lax.ppermute(mine, "z", [(i, (i + 1) % 8) for i in range(8)])
    after = lax.ppermute(mine, "z", [(i, (i - 1) % 8) for i in range(8)])
    cross = jnp.where(lax.axis_index("core") == 1, before, after)
    other = lax.ppermute(jnp.stack([mine, cross]), "core", [(0, 1), (1, 0)])
    return before, after, other


def on_device(features, mask, rulebook, weight_first, weight_second, cotangent):
    shape = jax.ShapeDtypeStruct
    x = lax.axis_index("x")
    core = lax.axis_index("core")
    here = lax.axis_index(SPACE)
    chan = lax.axis_index("chan")
    z = lax.axis_index("z")
    ids = jnp.stack([x, chan, core, (z == 0).astype(jnp.int32), (z == 7).astype(jnp.int32)]).astype(jnp.int32)
    swap = [(a * 4 + b, b * 4 + a) for a in range(4) for b in range(4)]

    shards = jnp.stack([weight_first, lax.ppermute(weight_second, ("x", "chan"), swap)])
    blocks = jnp.transpose(lax.all_gather(shards, ("z", "core"), axis=1, tiled=True), (0, 2, 1, 3))

    active = mask.astype(F32)[:, None]
    masked = (features.astype(F32) * active).astype(BF)
    grad_second = (cotangent.astype(F32) * active).astype(BF)

    padded = jnp.pad(rulebook.T, ((0, 5), (0, 0)), constant_values=-1)
    lane = np.arange(128)
    back_lane = np.where((lane >= 12) & (lane < 32), lane - 12, 0)
    read_by = np.where(lane < 12, lane // 6, back_lane % 2)
    reading = jnp.where(jnp.asarray(read_by == 0)[None], padded[:, 0:1], padded[:, 1:2])
    sources = np.array([0, 1, -2, -3, 2, 5])

    relative = jnp.where(reading >= 0, reading - here * 2, -(2**20))

    def lane_match(offsets, valid):
        target = np.where(valid, offsets, 2**20).astype(np.int32)
        return (relative == jnp.asarray(target)[None]).astype(BF)

    def back_match(position):
        valid = (lane >= 12) & (lane < 32) & (back_lane // 2 % 5 == position)
        step = 0 if position == 0 else STEPS[position - 1]
        return lane_match(2 * step + back_lane // 10, valid)

    compact = lane_match(sources[lane % 6], lane < 12)
    for position in range(5):
        compact = compact + back_match(position)
    packed = jnp.concatenate([masked[:64], grad_second, compact, masked[64:]], 0)
    turned = jnp.stack(
        [
            lax.ppermute(packed, ("x", "chan"), [(a * 4 + b, b * 4 + (a - r) % 4) for a in range(4) for b in range(4)])
            for r in range(4)
        ]
    )
    consts = tables()
    columns = shape((8, 9, 96, 128), BF)
    q_in, q_back, own, matched = call(
        gather_first,
        [columns, columns, shape((4, 128, 128), BF), shape((4, 32, 128), BF)],
        [],
        ids,
        turned,
        *spread_out(turned),
        *consts,
    )
    (partial,) = call(apply_first, [shape((4, 256, 128), F32)], [], q_in, q_back, blocks)
    summed = jnp.sum(lax.all_to_all(partial, "x", 0, 0, tiled=True), axis=0)
    first_act = active * summed[0:128]
    hidden_grad = summed[128:256]
    sigmoid_first = jax.nn.sigmoid(first_act)
    hidden = (first_act * sigmoid_first).astype(BF)
    grad_first = (
        active * hidden_grad * sigmoid_first * (1.0 + first_act * (1.0 - sigmoid_first))
    ).astype(BF)

    packed = jnp.concatenate([hidden, grad_first], 0)
    along = jnp.stack(
        [packed] + [lax.ppermute(packed, "x", [(a, (a - r) % 4) for a in range(4)]) for r in range(1, 4)]
    )
    pieces = shape((8, 27, 8, 128), F32)
    pair = pltpu.VMEM((2, 128, 128), F32)
    keep1, send1 = call(weigh_first, [pieces, pieces], [pltpu.VMEM((4, 128, 128), BF), pair], ids, along, q_in)
    reduced, keep2, send2 = call(
        apply_second,
        [shape((4, 256, 128), F32), pieces, pieces],
        [pltpu.VMEM((8, 9, 96, 128), BF), pltpu.VMEM((8, 9, 96, 128), BF), pair],
        ids,
        along,
        *spread_out(along),
        matched,
        own,
        blocks,
        *consts,
    )
    total = None
    for r in range(4):
        part = lax.ppermute(
            reduced[r], ("x", "chan"), [(a * 4 + b, (b + r) % 4 * 4 + a) for a in range(4) for b in range(4)]
        )
        total = part if total is None else total + part
    output = (active * total[0:128]).astype(BF)
    features_grad = (active * total[128:256]).astype(BF)

    def settle(keep, send):
        mine = keep + lax.ppermute(send, "core", [(0, 1), (1, 0)])
        moved = lax.all_to_all(mine.astype(BF).reshape(8, 27 * 8, 128), "z", 0, 0, tiled=True)
        return jnp.sum(moved.astype(F32), axis=0).reshape(27, 8, 128)

    second_sum = lax.ppermute(settle(keep2, send2), ("x", "chan"), swap)
    first_sum = settle(keep1, send1)
    return (
        output,
        features_grad,
        jnp.transpose(first_sum, (1, 0, 2)),
        jnp.transpose(second_sum, (1, 0, 2)),
    )


def solution(mesh):
    split = Mesh(mesh.devices.reshape(4, 8, 2, 4), ("x", "z", "core", "chan"))
    placed = (
        P(SPACE, "chan"),
        P(SPACE),
        P(SPACE, None),
        P(SPACE, None, "chan"),
        P(SPACE, None, "chan"),
        P(SPACE, "chan"),
    )
    return jax.shard_map(
        on_device,
        mesh=split,
        in_specs=placed,
        out_specs=(
            P(SPACE, "chan"),
            P(SPACE, "chan"),
            P(SPACE, None, "chan"),
            P(SPACE, None, "chan"),
        ),
        check_vma=False,
    )
```

```python
import jax
import jax.numpy as jnp
import numpy as np
from jax import lax
from jax.experimental import pallas as pl
from jax.experimental.pallas import tpu as pltpu
from jax.sharding import Mesh
from jax.sharding import PartitionSpec as P

STEPS = (1, 2, -1, -2)
SPACE = ("x", "z", "core")
CELLS = 224
BF = jnp.bfloat16
F32 = jnp.float32


def tables():
    pick = np.zeros((CELLS, 32), np.float32)
    pick_back = np.zeros((CELLS, 32), np.float32)
    local = np.zeros((CELLS, 128), np.float32)
    for row in range(216):
        cell = (row // 36, row // 6 % 6, row % 6)
        side = [(v == 5) - (v == 0) for v in cell]
        at = [(v - 1) % 4 for v in cell]
        pick[row, 9 * (side[0] + 1) + 3 * (side[1] + 1) + side[2] + 1] = 1
        pick_back[row, 9 * (1 - side[0]) + 3 * (1 - side[1]) + 1 - side[2]] = 1
        voxel = at[0] * 16 + at[1] * 4 + at[2]
        local[row, voxel] = 1
        local[row, 64 + voxel] = 1
    spread = np.zeros((9, 6, 4, 4, CELLS), np.float32)
    for move in range(9):
        for i in range(6):
            for j in range(4):
                for k in range(4):
                    spread[move, i, j, k, i * 36 + (j + move // 3) * 6 + k + move % 3] = 1
    lanes = np.zeros((128, 2048), np.float32)
    for brick in range(2):
        for column in range(384):
            lanes[brick * 6 + column // 64, brick * 384 + column] = 1
        for column in range(640):
            lanes[12 + brick * 10 + column // 64, 768 + brick * 640 + column] = 1
    lane = np.arange(128)
    device = np.where((lane >= 12) & (lane < 32), (lane - 12) % 10 // 2, 0)
    sources = np.zeros((16, 128), np.float32)
    sources[device, lane] = 1
    as_bf = lambda value: jnp.asarray(value, BF)
    return (
        as_bf(pick),
        as_bf(pick_back),
        jnp.asarray(local),
        as_bf(spread.reshape(864, CELLS)),
        as_bf(lanes),
        as_bf(sources),
    )


def dot(a, b):
    return jnp.dot(a, b, preferred_element_type=F32)


def fill(out, base, matches, rows, pick, local, spread):
    count = rows.shape[0]
    chosen = dot(pick, matches)
    select = (chosen * jnp.concatenate([local] * (count // 64), axis=1)).astype(BF)
    found = dot(jnp.concatenate([select[:, :count], select[:, count:]], axis=0), rows).astype(BF)
    wide = dot(spread, jnp.concatenate([found[:CELLS], found[CELLS:]], axis=1)).astype(BF)
    for brick in range(2):
        out[base + brick] = wide[:, brick * 128 : (brick + 1) * 128].reshape(9, 96, 128)


def block(ref, offset):
    start = offset // 9 * 16
    return ref[:, offset % 9, start : start + 64, :].reshape(512, 128)


def convolve(ref, weight):
    total = None
    for offset in range(27):
        part = dot(block(ref, offset), weight[offset])
        total = part if total is None else total + part
    return total


def convolve_back(ref, weight):
    total = None
    for offset in range(27):
        part = lax.dot_general(
            block(ref, 26 - offset), weight[offset], (((1,), (1,)), ((), ())), preferred_element_type=F32
        )
        total = part if total is None else total + part
    return total


def around(ids, own, before, after, other, turn):
    return (
        own.at[turn],
        other.at[1 - ids[2], (turn - ids[3] * (1 - ids[2])) & 3],
        before.at[(turn - ids[3]) & 3],
        other.at[ids[2], (turn + ids[4] * ids[2]) & 3],
        after.at[(turn + ids[4]) & 3],
    )


def gather_first(
    ids, mine, before, after, other, pick, pick_back, local, spread, lanes, sources, q_in, q_back, own, matched
):
    @pl.loop(0, 4)
    def _(turn):
        at = (ids[1] + turn) & 3
        views = around(ids, mine, before, after, other, turn)
        compact = None
        for device, view in enumerate(views):
            part = view[192:224, :] * sources[device : device + 1, :]
            compact = part if compact is None else compact + part
        matched[at] = compact
        own[at] = views[0][64:192, :]
        found = dot(compact, lanes[...]).astype(BF)
        rows = [views[0][0:64, :], views[0][224:288, :]]
        rows += [view[device % 2 * 224 : device % 2 * 224 + 64, :] for device, view in enumerate(views[1:])]
        fill(q_in, at * 2, found[:, :768], jnp.concatenate(rows, 0), pick[...], local[...], spread[...])
        rows = jnp.concatenate([view[64:192, :] for view in views], 0)
        fill(q_back, at * 2, found[:, 768:], rows, pick_back[...], local[...], spread[...])


def apply_first(q_in, q_back, weights, out):
    forward = convolve(q_in, weights.at[0])
    backward = convolve_back(q_back, weights.at[1])
    for at in range(4):
        out[at, 0:128, :] = forward[at * 128 : (at + 1) * 128]
        out[at, 128:256, :] = backward[at * 128 : (at + 1) * 128]


def weight_blocks(ref, gradient, keep, send, scratch, core):
    @pl.loop(0, 3)
    def _(move):
        start = pl.multiple_of(move * 16, 16)
        for rest in range(9):
            columns = ref[:, rest, pl.ds(start, 64), :].reshape(512, 128)
            scratch[rest % 2] = lax.dot_general(
                columns, gradient, (((0,), (0,)), ((), ())), preferred_element_type=F32
            )
            for z in range(8):
                keep[z, move * 9 + rest] = scratch[rest % 2, pl.ds(z * 16 + core * 8, 8), :]
                send[z, move * 9 + rest] = scratch[rest % 2, pl.ds(z * 16 + 8 - core * 8, 8), :]


def weigh_first(ids, mine, q_in, keep, send, own, scratch):
    for turn in range(4):
        own[(ids[0] + turn) & 3] = mine[turn, 128:256, :]
    weight_blocks(q_in, own[...].reshape(512, 128), keep, send, scratch, ids[2])


def weigh_second(
    ids, mine, before, after, other, matched, own, pick, pick_back, local, spread, lanes, sources,
    keep, send, q_hidden, scratch,
):
    @pl.loop(0, 4)
    def _(turn):
        at = (ids[0] + turn) & 3
        views = around(ids, mine, before, after, other, turn)
        found = dot(matched[at], lanes[:, :768]).astype(BF)
        rows = [views[0][0:128, :]]
        rows += [view[device % 2 * 64 : device % 2 * 64 + 64, :] for device, view in enumerate(views[1:])]
        fill(q_hidden, at * 2, found, jnp.concatenate(rows, 0), pick[...], local[...], spread[...])

    weight_blocks(q_hidden, own[...].reshape(512, 128), keep, send, scratch, ids[2])


def apply_second(
    ids, mine, before, after, other, matched, q_hidden, weights, pick, pick_back, local, spread, lanes, sources,
    reduced, q_back,
):
    @pl.loop(0, 4)
    def _(turn):
        at = (ids[0] + turn) & 3
        views = around(ids, mine, before, after, other, turn)
        found = dot(matched[at], lanes[:, 768:]).astype(BF)
        rows = jnp.concatenate([view[128:256, :] for view in views], 0)
        fill(q_back, at * 2, found, rows, pick_back[...], local[...], spread[...])

    forward = convolve(q_hidden, weights.at[1])
    backward = convolve_back(q_back, weights.at[0])
    for at in range(4):
        turn = (at - ids[1]) & 3
        reduced[turn, 0:128, :] = forward[at * 128 : (at + 1) * 128]
        reduced[turn, 128:256, :] = backward[at * 128 : (at + 1) * 128]


def call(kernel, outs, scratch, *args):
    smem = pl.BlockSpec(memory_space=pltpu.SMEM)
    vmem = pl.BlockSpec(memory_space=pltpu.VMEM)
    return pl.pallas_call(
        kernel,
        out_shape=outs,
        in_specs=[smem if value.dtype == jnp.int32 else vmem for value in args],
        out_specs=[vmem] * len(outs),
        scratch_shapes=scratch,
        compiler_params=pltpu.CompilerParams(vmem_limit_bytes=52 * 2**20),
    )(*args)


def turn_over(value, target):
    places = [(a, b) for a in range(4) for b in range(4)]
    moved = {place: tuple(v % 4 for v in target(*place)) for place in places}
    still = [place for place in places if moved[place] == place]
    for at, place in enumerate(still):
        moved[place] = still[(at + 1) % len(still)]
    came = lax.ppermute(value, ("x", "chan"), [(p[0] * 4 + p[1], q[0] * 4 + q[1]) for p, q in moved.items()])
    if not still:
        return came
    return jnp.where(lax.axis_index("x") == lax.axis_index("chan"), value, came)


def spread_out(mine):
    before = lax.ppermute(mine, "z", [(i, (i + 1) % 8) for i in range(8)])
    after = lax.ppermute(mine, "z", [(i, (i - 1) % 8) for i in range(8)])
    cross = jnp.where(lax.axis_index("core") == 1, before, after)
    other = lax.ppermute(jnp.stack([mine, cross]), "core", [(0, 1), (1, 0)])
    return before, after, other


def on_device(features, mask, rulebook, weight_first, weight_second, cotangent):
    shape = jax.ShapeDtypeStruct
    x = lax.axis_index("x")
    core = lax.axis_index("core")
    here = lax.axis_index(SPACE)
    chan = lax.axis_index("chan")
    z = lax.axis_index("z")
    ids = jnp.stack([x, chan, core, (z == 0).astype(jnp.int32), (z == 7).astype(jnp.int32)]).astype(jnp.int32)

    shards = jnp.stack([weight_first, turn_over(weight_second, lambda a, b: (b, a))])
    blocks = jnp.transpose(lax.all_gather(shards, ("z", "core"), axis=1, tiled=True), (0, 2, 1, 3))

    active = mask.astype(F32)[:, None]
    masked = (features.astype(F32) * active).astype(BF)
    grad_second = (cotangent.astype(F32) * active).astype(BF)

    padded = jnp.pad(rulebook.T, ((0, 5), (0, 0)), constant_values=-1)
    lane = np.arange(128)
    back_lane = np.where((lane >= 12) & (lane < 32), lane - 12, 0)
    read_by = np.where(lane < 12, lane // 6, back_lane % 2)
    reading = jnp.where(jnp.asarray(read_by == 0)[None], padded[:, 0:1], padded[:, 1:2])
    sources = np.array([0, 1, -2, -3, 2, 5])

    relative = jnp.where(reading >= 0, reading - here * 2, -(2**20))

    def lane_match(offsets, valid):
        target = np.where(valid, offsets, 2**20).astype(np.int32)
        return (relative == jnp.asarray(target)[None]).astype(BF)

    def back_match(position):
        valid = (lane >= 12) & (lane < 32) & (back_lane // 2 % 5 == position)
        step = 0 if position == 0 else STEPS[position - 1]
        return lane_match(2 * step + back_lane // 10, valid)

    compact = lane_match(sources[lane % 6], lane < 12)
    for position in range(5):
        compact = compact + back_match(position)
    packed = jnp.concatenate([masked[:64], grad_second, compact, masked[64:]], 0)
    turned = jnp.stack(
        [
            turn_over(packed, lambda a, b: (b, a - r))
            for r in range(4)
        ]
    )
    consts = tables()
    columns = shape((8, 9, 96, 128), BF)
    q_in, q_back, own, matched = call(
        gather_first,
        [columns, columns, shape((4, 128, 128), BF), shape((4, 32, 128), BF)],
        [],
        ids,
        turned,
        *spread_out(turned),
        *consts,
    )
    (partial,) = call(apply_first, [shape((4, 256, 128), F32)], [], q_in, q_back, blocks)
    summed = jnp.sum(lax.all_to_all(partial, "x", 0, 0, tiled=True), axis=0)
    first_act = active * summed[0:128]
    hidden_grad = summed[128:256]
    sigmoid_first = jax.nn.sigmoid(first_act)
    hidden = (first_act * sigmoid_first).astype(BF)
    grad_first = (
        active * hidden_grad * sigmoid_first * (1.0 + first_act * (1.0 - sigmoid_first))
    ).astype(BF)

    packed = jnp.concatenate([hidden, grad_first], 0)
    along = jnp.stack(
        [packed] + [lax.ppermute(packed, "x", [(a, (a - r) % 4) for a in range(4)]) for r in range(1, 4)]
    )
    pieces = shape((8, 27, 8, 128), F32)
    pair = pltpu.VMEM((2, 128, 128), F32)
    keep1, send1 = call(weigh_first, [pieces, pieces], [pltpu.VMEM((4, 128, 128), BF), pair], ids, along, q_in)

    def both_cores(keep, send):
        return keep + lax.ppermute(send, "core", [(0, 1), (1, 0)])

    first_mine = both_cores(keep1, send1)
    first_sum = lax.psum_scatter(first_mine, "z", scatter_dimension=0, tiled=True).reshape(27, 8, 128)
    before, after, other, _ = lax.optimization_barrier((*spread_out(along), first_mine))
    keep2, send2, q_hidden = call(
        weigh_second,
        [pieces, pieces, columns],
        [pair],
        ids,
        along,
        before,
        after,
        other,
        matched,
        own,
        *consts,
    )
    second_mine = both_cores(keep2, send2).astype(BF).reshape(8, 216, 128)
    q_hidden, second_mine = lax.optimization_barrier((q_hidden, second_mine))
    moved = lax.all_to_all(second_mine, "z", 0, 0, tiled=True)
    (reduced,) = call(
        apply_second,
        [shape((4, 256, 128), F32)],
        [pltpu.VMEM((8, 9, 96, 128), BF)],
        ids,
        along,
        before,
        after,
        other,
        matched,
        q_hidden,
        blocks,
        *consts,
    )
    total = None
    for r in range(4):
        part = turn_over(reduced[r], lambda a, b: (b + r, a))
        total = part if total is None else total + part
    output = (active * total[0:128]).astype(BF)
    features_grad = (active * total[128:256]).astype(BF)

    second_sum = turn_over(jnp.sum(moved.astype(F32), axis=0).reshape(27, 8, 128), lambda a, b: (b, a))
    return (
        output,
        features_grad,
        jnp.transpose(first_sum, (1, 0, 2)),
        jnp.transpose(second_sum, (1, 0, 2)),
    )


def solution(mesh):
    split = Mesh(mesh.devices.reshape(4, 8, 2, 4), ("x", "z", "core", "chan"))
    placed = (
        P(SPACE, "chan"),
        P(SPACE),
        P(SPACE, None),
        P(SPACE, None, "chan"),
        P(SPACE, None, "chan"),
        P(SPACE, "chan"),
    )
    return jax.shard_map(
        on_device,
        mesh=split,
        in_specs=placed,
        out_specs=(
            P(SPACE, "chan"),
            P(SPACE, "chan"),
            P(SPACE, None, "chan"),
            P(SPACE, None, "chan"),
        ),
        check_vma=False,
    )
```

```python
import jax
import jax.numpy as jnp
import numpy as np
from jax import lax
from jax.experimental import pallas as pl
from jax.experimental.pallas import tpu as pltpu
from jax.sharding import Mesh
from jax.sharding import PartitionSpec as P

STEPS = (1, 2, -1, -2)
SPACE = ("x", "z", "core")
CELLS = 224
BF = jnp.bfloat16
F32 = jnp.float32


def tables():
    pick = np.zeros((CELLS, 32), np.float32)
    pick_back = np.zeros((CELLS, 32), np.float32)
    local = np.zeros((CELLS, 128), np.float32)
    for row in range(216):
        cell = (row // 36, row // 6 % 6, row % 6)
        side = [(v == 5) - (v == 0) for v in cell]
        at = [(v - 1) % 4 for v in cell]
        pick[row, 9 * (side[0] + 1) + 3 * (side[1] + 1) + side[2] + 1] = 1
        pick_back[row, 9 * (1 - side[0]) + 3 * (1 - side[1]) + 1 - side[2]] = 1
        voxel = at[0] * 16 + at[1] * 4 + at[2]
        local[row, voxel] = 1
        local[row, 64 + voxel] = 1
    spread = np.zeros((9, 6, 4, 4, CELLS), np.float32)
    for move in range(9):
        for i in range(6):
            for j in range(4):
                for k in range(4):
                    spread[move, i, j, k, i * 36 + (j + move // 3) * 6 + k + move % 3] = 1
    lanes = np.zeros((128, 2048), np.float32)
    for brick in range(2):
        for column in range(384):
            lanes[brick * 6 + column // 64, brick * 384 + column] = 1
        for column in range(640):
            lanes[12 + brick * 10 + column // 64, 768 + brick * 640 + column] = 1
    lane = np.arange(128)
    device = np.where((lane >= 12) & (lane < 32), (lane - 12) % 10 // 2, 0)
    sources = np.zeros((16, 128), np.float32)
    sources[device, lane] = 1
    as_bf = lambda value: jnp.asarray(value, BF)
    return (
        as_bf(pick),
        as_bf(pick_back),
        jnp.asarray(local),
        as_bf(spread.reshape(864, CELLS)),
        as_bf(lanes),
        as_bf(sources),
    )


def dot(a, b):
    return jnp.dot(a, b, preferred_element_type=F32)


def fill(out, base, matches, rows, pick, local, spread):
    count = rows.shape[0]
    chosen = dot(pick, matches)
    select = (chosen * jnp.concatenate([local] * (count // 64), axis=1)).astype(BF)
    found = dot(jnp.concatenate([select[:, :count], select[:, count:]], axis=0), rows).astype(BF)
    wide = dot(spread, jnp.concatenate([found[:CELLS], found[CELLS:]], axis=1)).astype(BF)
    for brick in range(2):
        out[base + brick] = wide[:, brick * 128 : (brick + 1) * 128].reshape(9, 96, 128)


def block(ref, offset):
    start = offset // 9 * 16
    return ref[:, offset % 9, start : start + 64, :].reshape(512, 128)


def convolve(ref, weight):
    total = None
    for offset in range(27):
        part = dot(block(ref, offset), weight[offset])
        total = part if total is None else total + part
    return total


def convolve_back(ref, weight):
    total = None
    for offset in range(27):
        part = lax.dot_general(
            block(ref, 26 - offset), weight[offset], (((1,), (1,)), ((), ())), preferred_element_type=F32
        )
        total = part if total is None else total + part
    return total


def around(ids, own, before, after, other, turn):
    return (
        own.at[turn],
        other.at[1 - ids[2], (turn - ids[3] * (1 - ids[2])) & 3],
        before.at[(turn - ids[3]) & 3],
        other.at[ids[2], (turn + ids[4] * ids[2]) & 3],
        after.at[(turn + ids[4]) & 3],
    )


def gather_first(
    ids, mine, before, after, other, pick, pick_back, local, spread, lanes, sources, q_in, q_back, own, matched
):
    @pl.loop(0, 4, unroll=2)
    def _(turn):
        at = (ids[1] + turn) & 3
        views = around(ids, mine, before, after, other, turn)
        compact = None
        for device, view in enumerate(views):
            part = view[192:224, :] * sources[device : device + 1, :]
            compact = part if compact is None else compact + part
        matched[at] = compact
        own[at] = views[0][64:192, :]
        found = dot(compact, lanes[...]).astype(BF)
        rows = [views[0][0:64, :], views[0][224:288, :]]
        rows += [view[device % 2 * 224 : device % 2 * 224 + 64, :] for device, view in enumerate(views[1:])]
        fill(q_in, at * 2, found[:, :768], jnp.concatenate(rows, 0), pick[...], local[...], spread[...])
        rows = jnp.concatenate([view[64:192, :] for view in views], 0)
        fill(q_back, at * 2, found[:, 768:], rows, pick_back[...], local[...], spread[...])


def apply_first(ids, q_in, q_back, weights, out):
    forward = convolve(q_in, weights.at[0])
    backward = convolve_back(q_back, weights.at[1])
    for at in range(4):
        turn = (at - ids[0]) & 3
        out[turn, 0:128, :] = forward[at * 128 : (at + 1) * 128]
        out[turn, 128:256, :] = backward[at * 128 : (at + 1) * 128]


def weight_blocks(ref, gradient, keep, send, scratch, core):
    turned = gradient.T

    @pl.loop(0, 3)
    def _(side):
        for step in range(3):
            rest = side * 3 + step
            columns = [ref[:, rest, move * 16 : move * 16 + 64, :].reshape(512, 128) for move in range(3)]
            found = dot(turned, jnp.concatenate(columns, 1))
            for move in range(3):
                scratch[step % 2, move * 128 : (move + 1) * 128] = found[:, move * 128 : (move + 1) * 128].T
                for z in range(8):
                    start = move * 128 + z * 16
                    keep[z, move * 9 + rest] = scratch[step % 2, pl.ds(start + core * 8, 8), :]
                    send[z, move * 9 + rest] = scratch[step % 2, pl.ds(start + 8 - core * 8, 8), :]


def weigh_first(ids, mine, q_in, keep, send, own, scratch):
    for turn in range(4):
        own[(ids[0] + turn) & 3] = mine[turn, 128:256, :]
    weight_blocks(q_in, own[...].reshape(512, 128), keep, send, scratch, ids[2])


def weigh_second(
    ids, mine, before, after, other, matched, own, pick, pick_back, local, spread, lanes, sources,
    keep, send, q_hidden, scratch,
):
    @pl.loop(0, 4, unroll=2)
    def _(turn):
        at = (ids[0] + turn) & 3
        views = around(ids, mine, before, after, other, turn)
        found = dot(matched[at], lanes[:, :768]).astype(BF)
        rows = [views[0][0:128, :]]
        rows += [view[device % 2 * 64 : device % 2 * 64 + 64, :] for device, view in enumerate(views[1:])]
        fill(q_hidden, at * 2, found, jnp.concatenate(rows, 0), pick[...], local[...], spread[...])

    weight_blocks(q_hidden, own[...].reshape(512, 128), keep, send, scratch, ids[2])


def apply_second(
    ids, mine, before, after, other, matched, q_hidden, weights, pick, pick_back, local, spread, lanes, sources,
    reduced, q_back,
):
    @pl.loop(0, 4, unroll=2)
    def _(turn):
        at = (ids[0] + turn) & 3
        views = around(ids, mine, before, after, other, turn)
        found = dot(matched[at], lanes[:, 768:]).astype(BF)
        rows = jnp.concatenate([view[128:256, :] for view in views], 0)
        fill(q_back, at * 2, found, rows, pick_back[...], local[...], spread[...])

    forward = convolve(q_hidden, weights.at[1])
    backward = convolve_back(q_back, weights.at[0])
    for at in range(4):
        turn = (at - ids[1]) & 3
        reduced[turn, 0:128, :] = forward[at * 128 : (at + 1) * 128]
        reduced[turn, 128:256, :] = backward[at * 128 : (at + 1) * 128]


def call(kernel, outs, scratch, *args):
    smem = pl.BlockSpec(memory_space=pltpu.SMEM)
    vmem = pl.BlockSpec(memory_space=pltpu.VMEM)
    return pl.pallas_call(
        kernel,
        out_shape=outs,
        in_specs=[smem if value.dtype == jnp.int32 else vmem for value in args],
        out_specs=[vmem] * len(outs),
        scratch_shapes=scratch,
        compiler_params=pltpu.CompilerParams(vmem_limit_bytes=52 * 2**20),
    )(*args)


def turn_over(value, target):
    places = [(a, b) for a in range(4) for b in range(4)]
    moved = {place: tuple(v % 4 for v in target(*place)) for place in places}
    still = [place for place in places if moved[place] == place]
    for at, place in enumerate(still):
        moved[place] = still[(at + 1) % len(still)]
    came = lax.ppermute(value, ("x", "chan"), [(p[0] * 4 + p[1], q[0] * 4 + q[1]) for p, q in moved.items()])
    if not still:
        return came
    return jnp.where(lax.axis_index("x") == lax.axis_index("chan"), value, came)


def spread_out(mine):
    before = lax.ppermute(mine, "z", [(i, (i + 1) % 8) for i in range(8)])
    after = lax.ppermute(mine, "z", [(i, (i - 1) % 8) for i in range(8)])
    cross = jnp.where(lax.axis_index("core") == 1, before, after)
    other = lax.ppermute(jnp.stack([mine, cross]), "core", [(0, 1), (1, 0)])
    return before, after, other


def on_device(features, mask, rulebook, weight_first, weight_second, cotangent):
    shape = jax.ShapeDtypeStruct
    x = lax.axis_index("x")
    core = lax.axis_index("core")
    here = lax.axis_index(SPACE)
    chan = lax.axis_index("chan")
    z = lax.axis_index("z")
    ids = jnp.stack([x, chan, core, (z == 0).astype(jnp.int32), (z == 7).astype(jnp.int32)]).astype(jnp.int32)

    shards = jnp.stack([weight_first, turn_over(weight_second, lambda a, b: (b, a))])
    blocks = jnp.transpose(lax.all_gather(shards, ("z", "core"), axis=1, tiled=True), (0, 2, 1, 3))

    active = mask.astype(F32)[:, None]
    masked = (features.astype(F32) * active).astype(BF)
    grad_second = (cotangent.astype(F32) * active).astype(BF)

    padded = jnp.pad(rulebook.T, ((0, 5), (0, 0)), constant_values=-1)
    lane = np.arange(128)
    back_lane = np.where((lane >= 12) & (lane < 32), lane - 12, 0)
    read_by = np.where(lane < 12, lane // 6, back_lane % 2)
    reading = jnp.where(jnp.asarray(read_by == 0)[None], padded[:, 0:1], padded[:, 1:2])
    sources = np.array([0, 1, -2, -3, 2, 5])

    relative = jnp.where(reading >= 0, reading - here * 2, -(2**20))

    def lane_match(offsets, valid):
        target = np.where(valid, offsets, 2**20).astype(np.int32)
        return (relative == jnp.asarray(target)[None]).astype(BF)

    def back_match(position):
        valid = (lane >= 12) & (lane < 32) & (back_lane // 2 % 5 == position)
        step = 0 if position == 0 else STEPS[position - 1]
        return lane_match(2 * step + back_lane // 10, valid)

    compact = lane_match(sources[lane % 6], lane < 12)
    for position in range(5):
        compact = compact + back_match(position)
    packed = jnp.concatenate([masked[:64], grad_second, compact, masked[64:]], 0)
    turned = jnp.stack(
        [
            turn_over(packed, lambda a, b: (b, a - r))
            for r in range(4)
        ]
    )
    consts = tables()
    columns = shape((8, 9, 96, 128), BF)
    q_in, q_back, own, matched = call(
        gather_first,
        [columns, columns, shape((4, 128, 128), BF), shape((4, 32, 128), BF)],
        [],
        ids,
        turned,
        *spread_out(turned),
        *consts,
    )
    (partial,) = call(apply_first, [shape((4, 256, 128), F32)], [], ids, q_in, q_back, blocks)
    summed = partial[0]
    for r in range(1, 4):
        summed = summed + lax.ppermute(partial[r], "x", [(a, (a + r) % 4) for a in range(4)])
    first_act = active * summed[0:128]
    hidden_grad = summed[128:256]
    sigmoid_first = jax.nn.sigmoid(first_act)
    hidden = (first_act * sigmoid_first).astype(BF)
    grad_first = (
        active * hidden_grad * sigmoid_first * (1.0 + first_act * (1.0 - sigmoid_first))
    ).astype(BF)

    packed = jnp.concatenate([hidden, grad_first], 0)
    along = jnp.stack(
        [packed] + [lax.ppermute(packed, "x", [(a, (a - r) % 4) for a in range(4)]) for r in range(1, 4)]
    )
    pieces = shape((8, 27, 8, 128), F32)
    pair = pltpu.VMEM((2, 384, 128), F32)
    keep1, send1 = call(weigh_first, [pieces, pieces], [pltpu.VMEM((4, 128, 128), BF), pair], ids, along, q_in)

    def both_cores(keep, send):
        return keep + lax.ppermute(send, "core", [(0, 1), (1, 0)])

    first_mine = both_cores(keep1, send1)
    first_sum = lax.psum_scatter(first_mine, "z", scatter_dimension=0, tiled=True).reshape(27, 8, 128)
    before, after, other, _ = lax.optimization_barrier((*spread_out(along), first_mine))
    keep2, send2, q_hidden = call(
        weigh_second,
        [pieces, pieces, columns],
        [pair],
        ids,
        along,
        before,
        after,
        other,
        matched,
        own,
        *consts,
    )
    second_mine = both_cores(keep2, send2).astype(BF).reshape(8, 216, 128)
    q_hidden, second_mine = lax.optimization_barrier((q_hidden, second_mine))
    moved = lax.all_to_all(second_mine, "z", 0, 0, tiled=True)
    (reduced,) = call(
        apply_second,
        [shape((4, 256, 128), F32)],
        [pltpu.VMEM((8, 9, 96, 128), BF)],
        ids,
        along,
        before,
        after,
        other,
        matched,
        q_hidden,
        blocks,
        *consts,
    )
    parts = [turn_over(reduced[r], lambda a, b: (b + r, a)) for r in range(4)]
    second_sum = jnp.sum(moved.astype(F32), axis=0).reshape(27, 8, 128)
    *parts, _ = lax.optimization_barrier((*parts, second_sum))
    second_sum = turn_over(second_sum, lambda a, b: (b, a))
    total = parts[0] + parts[1] + parts[2] + parts[3]
    output = (active * total[0:128]).astype(BF)
    features_grad = (active * total[128:256]).astype(BF)

    return (
        output,
        features_grad,
        jnp.transpose(first_sum, (1, 0, 2)),
        jnp.transpose(second_sum, (1, 0, 2)),
    )


def solution(mesh):
    split = Mesh(mesh.devices.reshape(4, 8, 2, 4), ("x", "z", "core", "chan"))
    placed = (
        P(SPACE, "chan"),
        P(SPACE),
        P(SPACE, None),
        P(SPACE, None, "chan"),
        P(SPACE, None, "chan"),
        P(SPACE, "chan"),
    )
    return jax.shard_map(
        on_device,
        mesh=split,
        in_specs=placed,
        out_specs=(
            P(SPACE, "chan"),
            P(SPACE, "chan"),
            P(SPACE, None, "chan"),
            P(SPACE, None, "chan"),
        ),
        check_vma=False,
    )
```

```python
import jax
import jax.numpy as jnp
import numpy as np
from jax import lax
from jax.experimental import pallas as pl
from jax.experimental.pallas import tpu as pltpu
from jax.sharding import Mesh
from jax.sharding import PartitionSpec as P

STEPS = (1, 2, -1, -2)
SPACE = ("x", "z", "core")
CELLS = 224
EARLY = 24
BF = jnp.bfloat16
F32 = jnp.float32


def tables():
    pick = np.zeros((CELLS, 32), np.float32)
    pick_back = np.zeros((CELLS, 32), np.float32)
    local = np.zeros((CELLS, 128), np.float32)
    for row in range(216):
        cell = (row // 36, row // 6 % 6, row % 6)
        side = [(v == 5) - (v == 0) for v in cell]
        at = [(v - 1) % 4 for v in cell]
        pick[row, 9 * (side[0] + 1) + 3 * (side[1] + 1) + side[2] + 1] = 1
        pick_back[row, 9 * (1 - side[0]) + 3 * (1 - side[1]) + 1 - side[2]] = 1
        voxel = at[0] * 16 + at[1] * 4 + at[2]
        local[row, voxel] = 1
        local[row, 64 + voxel] = 1
    spread = np.zeros((9, 6, 4, 4, CELLS), np.float32)
    for move in range(9):
        for i in range(6):
            for j in range(4):
                for k in range(4):
                    spread[move, i, j, k, i * 36 + (j + move // 3) * 6 + k + move % 3] = 1
    lanes = np.zeros((32, 2048), np.float32)
    for brick in range(2):
        for column in range(384):
            lanes[brick * 6 + column // 64, brick * 384 + column] = 1
        for column in range(640):
            lanes[12 + brick * 10 + column // 64, 768 + brick * 640 + column] = 1
    lane = np.arange(128)
    device = np.where((lane >= 12) & (lane < 32), (lane - 12) % 10 // 2, 0)
    sources = np.zeros((16, 128), np.float32)
    sources[device, lane] = 1
    as_bf = lambda value: jnp.asarray(value, BF)
    return (
        as_bf(pick),
        as_bf(pick_back),
        jnp.asarray(local),
        as_bf(spread.reshape(864, CELLS)),
        as_bf(lanes),
        as_bf(sources),
    )


def dot(a, b):
    return jnp.dot(a, b, preferred_element_type=F32)


def fill(out, base, matches, rows, pick, local, spread):
    count = rows.shape[0]
    chosen = dot(pick, matches)
    select = (chosen * jnp.concatenate([local] * (count // 64), axis=1)).astype(BF)
    found = dot(jnp.concatenate([select[:, :count], select[:, count:]], axis=0), rows).astype(BF)
    wide = dot(spread, jnp.concatenate([found[:CELLS], found[CELLS:]], axis=1)).astype(BF)
    for brick in range(2):
        out[base + brick] = wide[:, brick * 128 : (brick + 1) * 128].reshape(9, 96, 128)


def block(ref, offset):
    start = offset // 9 * 16
    return ref[:, offset % 9, start : start + 64, :].reshape(512, 128)


def convolve(ref, weight):
    total = None
    for offset in range(27):
        part = dot(block(ref, offset), weight[offset])
        total = part if total is None else total + part
    return total


def convolve_back(ref, weight):
    total = None
    for offset in range(27):
        part = lax.dot_general(
            block(ref, 26 - offset), weight[offset], (((1,), (1,)), ((), ())), preferred_element_type=F32
        )
        total = part if total is None else total + part
    return total


def around(ids, own, before, after, other, turn):
    return (
        own.at[turn],
        other.at[1 - ids[2], (turn - ids[3] * (1 - ids[2])) & 3],
        before.at[(turn - ids[3]) & 3],
        other.at[ids[2], (turn + ids[4] * ids[2]) & 3],
        after.at[(turn + ids[4]) & 3],
    )


def gather_first(
    ids, mine, before, after, other, pick, pick_back, local, spread, lanes, sources, q_in, q_back, own, matched
):
    @pl.loop(0, 4, unroll=2)
    def _(turn):
        at = (ids[1] + turn) & 3
        views = around(ids, mine, before, after, other, turn)
        compact = None
        for device, view in enumerate(views):
            part = view[192:224, :] * sources[device : device + 1, :]
            compact = part if compact is None else compact + part
        matched[at] = compact
        own[at] = views[0][64:192, :]
        found = dot(compact[:, :32], lanes[...]).astype(BF)
        rows = [views[0][0:64, :], views[0][224:288, :]]
        rows += [view[device % 2 * 224 : device % 2 * 224 + 64, :] for device, view in enumerate(views[1:])]
        fill(q_in, at * 2, found[:, :768], jnp.concatenate(rows, 0), pick[...], local[...], spread[...])
        rows = jnp.concatenate([view[64:192, :] for view in views], 0)
        fill(q_back, at * 2, found[:, 768:], rows, pick_back[...], local[...], spread[...])


def apply_first(ids, q_in, q_back, weights, out):
    forward = convolve(q_in, weights.at[0])
    backward = convolve_back(q_back, weights.at[1])
    for at in range(4):
        turn = (at - ids[0]) & 3
        out[turn, 0:128, :] = forward[at * 128 : (at + 1) * 128]
        out[turn, 128:256, :] = backward[at * 128 : (at + 1) * 128]


def weight_blocks(ref, gradient, keep, send, scratch, core):
    turned = gradient.T

    @pl.loop(0, 3)
    def _(side):
        for step in range(3):
            rest = side * 3 + step
            columns = [ref[:, rest, move * 16 : move * 16 + 64, :].reshape(512, 128) for move in range(3)]
            found = dot(turned, jnp.concatenate(columns, 1))
            for move in range(3):
                scratch[step % 2, move * 128 : (move + 1) * 128] = found[:, move * 128 : (move + 1) * 128].T
                for z in range(8):
                    start = move * 128 + z * 16
                    keep[z, move * 9 + rest] = scratch[step % 2, pl.ds(start + core * 8, 8), :]
                    send[z, move * 9 + rest] = scratch[step % 2, pl.ds(start + 8 - core * 8, 8), :]


def weigh_first(ids, mine, q_in, keep, send, own, scratch):
    for turn in range(4):
        own[(ids[0] + turn) & 3] = mine[turn, 128:256, :]
    weight_blocks(q_in, own[...].reshape(512, 128), keep, send, scratch, ids[2])


def weigh_second(
    ids, mine, before, after, other, matched, own, pick, pick_back, local, spread, lanes, sources,
    keep, send, q_hidden, scratch,
):
    @pl.loop(0, 4, unroll=2)
    def _(turn):
        at = (ids[0] + turn) & 3
        views = around(ids, mine, before, after, other, turn)
        found = dot(matched[at, :, :32], lanes[:, :768]).astype(BF)
        rows = [views[0][0:128, :]]
        rows += [view[device % 2 * 64 : device % 2 * 64 + 64, :] for device, view in enumerate(views[1:])]
        fill(q_hidden, at * 2, found, jnp.concatenate(rows, 0), pick[...], local[...], spread[...])

    weight_blocks(q_hidden, own[...].reshape(512, 128), keep, send, scratch, ids[2])


def apply_second(
    ids, mine, before, after, other, matched, q_hidden, weights, pick, pick_back, local, spread, lanes, sources,
    reduced, q_back,
):
    @pl.loop(0, 4, unroll=2)
    def _(turn):
        at = (ids[0] + turn) & 3
        views = around(ids, mine, before, after, other, turn)
        found = dot(matched[at, :, :32], lanes[:, 768:]).astype(BF)
        rows = jnp.concatenate([view[128:256, :] for view in views], 0)
        fill(q_back, at * 2, found, rows, pick_back[...], local[...], spread[...])

    forward = convolve(q_hidden, weights.at[1])
    backward = convolve_back(q_back, weights.at[0])
    for at in range(4):
        turn = (at - ids[1]) & 3
        reduced[turn, 0:128, :] = forward[at * 128 : (at + 1) * 128]
        reduced[turn, 128:256, :] = backward[at * 128 : (at + 1) * 128]


def call(kernel, outs, scratch, *args):
    smem = pl.BlockSpec(memory_space=pltpu.SMEM)
    vmem = pl.BlockSpec(memory_space=pltpu.VMEM)
    return pl.pallas_call(
        kernel,
        out_shape=outs,
        in_specs=[smem if value.dtype == jnp.int32 else vmem for value in args],
        out_specs=[vmem] * len(outs),
        scratch_shapes=scratch,
        compiler_params=pltpu.CompilerParams(vmem_limit_bytes=52 * 2**20),
    )(*args)


def turn_over(value, target):
    places = [(a, b) for a in range(4) for b in range(4)]
    moved = {place: tuple(v % 4 for v in target(*place)) for place in places}
    still = [place for place in places if moved[place] == place]
    for at, place in enumerate(still):
        moved[place] = still[(at + 1) % len(still)]
    came = lax.ppermute(value, ("x", "chan"), [(p[0] * 4 + p[1], q[0] * 4 + q[1]) for p, q in moved.items()])
    return (value, came) if still else (came, came)


def settled(value, came):
    return came if value is came else jnp.where(lax.axis_index("x") == lax.axis_index("chan"), value, came)


def spread_out(mine):
    before = lax.ppermute(mine, "z", [(i, (i + 1) % 8) for i in range(8)])
    after = lax.ppermute(mine, "z", [(i, (i - 1) % 8) for i in range(8)])
    cross = jnp.where(lax.axis_index("core") == 1, before, after)
    other = lax.ppermute(jnp.stack([mine, cross]), "core", [(0, 1), (1, 0)])
    return before, after, other


def on_device(features, mask, rulebook, weight_first, weight_second, cotangent):
    shape = jax.ShapeDtypeStruct
    x = lax.axis_index("x")
    core = lax.axis_index("core")
    here = lax.axis_index(SPACE)
    chan = lax.axis_index("chan")
    z = lax.axis_index("z")
    ids = jnp.stack([x, chan, core, (z == 0).astype(jnp.int32), (z == 7).astype(jnp.int32)]).astype(jnp.int32)

    shards = jnp.stack([weight_first, settled(*turn_over(weight_second, lambda a, b: (b, a)))])
    blocks = jnp.transpose(lax.all_gather(shards, ("z", "core"), axis=1, tiled=True), (0, 2, 1, 3))

    active = mask.astype(F32)[:, None]
    masked = (features.astype(F32) * active).astype(BF)
    grad_second = (cotangent.astype(F32) * active).astype(BF)

    padded = jnp.pad(rulebook.T, ((0, 5), (0, 0)), constant_values=-1)
    lane = np.arange(128)
    back_lane = np.where((lane >= 12) & (lane < 32), lane - 12, 0)
    read_by = np.where(lane < 12, lane // 6, back_lane % 2)
    reading = jnp.where(jnp.asarray(read_by == 0)[None], padded[:, 0:1], padded[:, 1:2])
    sources = np.array([0, 1, -2, -3, 2, 5])

    relative = jnp.where(reading >= 0, reading - here * 2, -(2**20))

    def lane_match(offsets, valid):
        target = np.where(valid, offsets, 2**20).astype(np.int32)
        return (relative == jnp.asarray(target)[None]).astype(BF)

    def back_match(position):
        valid = (lane >= 12) & (lane < 32) & (back_lane // 2 % 5 == position)
        step = 0 if position == 0 else STEPS[position - 1]
        return lane_match(2 * step + back_lane // 10, valid)

    compact = lane_match(sources[lane % 6], lane < 12)
    for position in range(5):
        compact = compact + back_match(position)
    packed = jnp.concatenate([masked[:64], grad_second, compact, masked[64:]], 0)
    turned = jnp.stack(
        [
            settled(*turn_over(packed, lambda a, b: (b, a - r)))
            for r in range(4)
        ]
    )
    consts = tables()
    columns = shape((8, 9, 96, 128), BF)
    q_in, q_back, own, matched = call(
        gather_first,
        [columns, columns, shape((4, 128, 128), BF), shape((4, 32, 128), BF)],
        [],
        ids,
        turned,
        *spread_out(turned),
        *consts,
    )
    (partial,) = call(apply_first, [shape((4, 256, 128), F32)], [], ids, q_in, q_back, blocks)
    summed = partial[0]
    for r in range(1, 4):
        summed = summed + lax.ppermute(partial[r], "x", [(a, (a + r) % 4) for a in range(4)])
    first_act = active * summed[0:128]
    hidden_grad = summed[128:256]
    sigmoid_first = jax.nn.sigmoid(first_act)
    hidden = (first_act * sigmoid_first).astype(BF)
    grad_first = (
        active * hidden_grad * sigmoid_first * (1.0 + first_act * (1.0 - sigmoid_first))
    ).astype(BF)

    packed = jnp.concatenate([hidden, grad_first], 0)
    along = jnp.stack(
        [packed] + [lax.ppermute(packed, "x", [(a, (a - r) % 4) for a in range(4)]) for r in range(1, 4)]
    )
    pieces = shape((8, 27, 8, 128), F32)
    pair = pltpu.VMEM((2, 384, 128), F32)
    keep1, send1 = call(weigh_first, [pieces, pieces], [pltpu.VMEM((4, 128, 128), BF), pair], ids, along, q_in)

    def both_cores(keep, send):
        return keep + lax.ppermute(send, "core", [(0, 1), (1, 0)])

    first_mine = both_cores(keep1, send1)
    first_early = first_mine[:, :EARLY]
    first_sum = lax.psum_scatter(first_early, "z", scatter_dimension=0, tiled=True).reshape(EARLY, 8, 128)
    before, after, other, _ = lax.optimization_barrier((*spread_out(along), first_early))
    keep2, send2, q_hidden = call(
        weigh_second,
        [pieces, pieces, columns],
        [pair],
        ids,
        along,
        before,
        after,
        other,
        matched,
        own,
        *consts,
    )
    second_mine = jnp.concatenate([both_cores(keep2, send2).astype(BF), first_mine[:, EARLY:].astype(BF)], 1)
    second_mine = second_mine.reshape(8, -1, 128)
    q_hidden, second_mine = lax.optimization_barrier((q_hidden, second_mine))
    moved = lax.all_to_all(second_mine, "z", 0, 0, tiled=True)
    (reduced,) = call(
        apply_second,
        [shape((4, 256, 128), F32)],
        [pltpu.VMEM((8, 9, 96, 128), BF)],
        ids,
        along,
        before,
        after,
        other,
        matched,
        q_hidden,
        blocks,
        *consts,
    )
    parts = [turn_over(reduced[r], lambda a, b: (b + r, a)) for r in range(4)]
    sums = jnp.sum(moved.astype(F32), axis=0).reshape(-1, 8, 128)
    second_sum = settled(*turn_over(sums[:27], lambda a, b: (b, a)))
    first_sum = jnp.concatenate([first_sum, sums[27:]], 0)
    *came, _ = lax.optimization_barrier((*(part[1] for part in parts), second_sum))
    total = settled(parts[0][0], came[0]) + came[1] + came[2] + came[3]
    output = (active * total[0:128]).astype(BF)
    features_grad = (active * total[128:256]).astype(BF)

    return (
        output,
        features_grad,
        jnp.transpose(first_sum, (1, 0, 2)),
        jnp.transpose(second_sum, (1, 0, 2)),
    )


def solution(mesh):
    split = Mesh(mesh.devices.reshape(4, 8, 2, 4), ("x", "z", "core", "chan"))
    placed = (
        P(SPACE, "chan"),
        P(SPACE),
        P(SPACE, None),
        P(SPACE, None, "chan"),
        P(SPACE, None, "chan"),
        P(SPACE, "chan"),
    )
    return jax.shard_map(
        on_device,
        mesh=split,
        in_specs=placed,
        out_specs=(
            P(SPACE, "chan"),
            P(SPACE, "chan"),
            P(SPACE, None, "chan"),
            P(SPACE, None, "chan"),
        ),
        check_vma=False,
    )
```

```python
import jax
import jax.numpy as jnp
import numpy as np
from jax import lax
from jax.experimental import pallas as pl
from jax.experimental.pallas import tpu as pltpu
from jax.sharding import Mesh
from jax.sharding import PartitionSpec as P

STEPS = (1, 2, -1, -2)
SPACE = ("x", "z", "core")
CELLS = 224
BF = jnp.bfloat16
F32 = jnp.float32


def tables():
    pick = np.zeros((CELLS, 32), np.float32)
    pick_back = np.zeros((CELLS, 32), np.float32)
    local = np.zeros((CELLS, 128), np.float32)
    for row in range(216):
        cell = (row // 36, row // 6 % 6, row % 6)
        side = [(v == 5) - (v == 0) for v in cell]
        at = [(v - 1) % 4 for v in cell]
        pick[row, 9 * (side[0] + 1) + 3 * (side[1] + 1) + side[2] + 1] = 1
        pick_back[row, 9 * (1 - side[0]) + 3 * (1 - side[1]) + 1 - side[2]] = 1
        voxel = at[0] * 16 + at[1] * 4 + at[2]
        local[row, voxel] = 1
        local[row, 64 + voxel] = 1
    spread = np.zeros((9, 6, 4, 4, CELLS), np.float32)
    for move in range(9):
        for i in range(6):
            for j in range(4):
                for k in range(4):
                    spread[move, i, j, k, i * 36 + (j + move // 3) * 6 + k + move % 3] = 1
    lanes = np.zeros((32, 2048), np.float32)
    for brick in range(2):
        for column in range(384):
            lanes[brick * 6 + column // 64, brick * 384 + column] = 1
        for column in range(640):
            lanes[12 + brick * 10 + column // 64, 768 + brick * 640 + column] = 1
    lane = np.arange(128)
    device = np.where((lane >= 12) & (lane < 32), (lane - 12) % 10 // 2, 0)
    sources = np.zeros((16, 128), np.float32)
    sources[device, lane] = 1
    as_bf = lambda value: jnp.asarray(value, BF)
    return (
        as_bf(pick),
        as_bf(pick_back),
        jnp.asarray(local),
        as_bf(spread.reshape(864, CELLS)),
        as_bf(lanes),
        as_bf(sources),
    )


def dot(a, b):
    return jnp.dot(a, b, preferred_element_type=F32)


def fill(out, base, matches, rows, pick, local, spread):
    count = rows.shape[0]
    chosen = dot(pick, matches)
    select = (chosen * jnp.concatenate([local] * (count // 64), axis=1)).astype(BF)
    found = dot(jnp.concatenate([select[:, :count], select[:, count:]], axis=0), rows).astype(BF)
    wide = dot(spread, jnp.concatenate([found[:CELLS], found[CELLS:]], axis=1)).astype(BF)
    for brick in range(2):
        out[base + brick] = wide[:, brick * 128 : (brick + 1) * 128].reshape(9, 96, 128)


def block(ref, offset):
    start = offset // 9 * 16
    return ref[:, offset % 9, start : start + 64, :].reshape(512, 128)


def convolve(ref, weight):
    total = None
    for offset in range(27):
        part = dot(block(ref, offset), weight[offset])
        total = part if total is None else total + part
    return total


def convolve_back(ref, weight):
    total = None
    for offset in range(27):
        part = lax.dot_general(
            block(ref, 26 - offset), weight[offset], (((1,), (1,)), ((), ())), preferred_element_type=F32
        )
        total = part if total is None else total + part
    return total


def around(ids, own, before, after, other, turn):
    return (
        own.at[turn],
        other.at[1 - ids[2], (turn - ids[3] * (1 - ids[2])) & 3],
        before.at[(turn - ids[3]) & 3],
        other.at[ids[2], (turn + ids[4] * ids[2]) & 3],
        after.at[(turn + ids[4]) & 3],
    )


def gather_first(
    ids, mine, before, after, other, pick, pick_back, local, spread, lanes, sources, q_in, q_back, own, matched
):
    @pl.loop(0, 4, unroll=2)
    def _(turn):
        at = (ids[1] + turn) & 3
        views = around(ids, mine, before, after, other, turn)
        compact = None
        for device, view in enumerate(views):
            part = view[192:224, :] * sources[device : device + 1, :]
            compact = part if compact is None else compact + part
        matched[at] = compact
        own[at] = views[0][64:192, :]
        found = dot(compact[:, :32], lanes[...]).astype(BF)
        rows = [views[0][0:64, :], views[0][224:288, :]]
        rows += [view[device % 2 * 224 : device % 2 * 224 + 64, :] for device, view in enumerate(views[1:])]
        fill(q_in, at * 2, found[:, :768], jnp.concatenate(rows, 0), pick[...], local[...], spread[...])
        rows = jnp.concatenate([view[64:192, :] for view in views], 0)
        fill(q_back, at * 2, found[:, 768:], rows, pick_back[...], local[...], spread[...])


def apply_first(ids, q_in, q_back, weights, out):
    forward = convolve(q_in, weights.at[0])
    backward = convolve_back(q_back, weights.at[1])
    for at in range(4):
        turn = (at - ids[0]) & 3
        out[turn, 0:128, :] = forward[at * 128 : (at + 1) * 128]
        out[turn, 128:256, :] = backward[at * 128 : (at + 1) * 128]


def weight_blocks(ref, gradient, keep, send, scratch, core):
    turned = gradient.T

    @pl.loop(0, 3)
    def _(side):
        for step in range(3):
            rest = side * 3 + step
            columns = [ref[:, rest, move * 16 : move * 16 + 64, :].reshape(512, 128) for move in range(3)]
            found = dot(turned, jnp.concatenate(columns, 1))
            for move in range(3):
                scratch[step % 2, move * 128 : (move + 1) * 128] = found[:, move * 128 : (move + 1) * 128].T
                for z in range(8):
                    start = move * 128 + z * 16
                    keep[z, move * 9 + rest] = scratch[step % 2, pl.ds(start + core * 8, 8), :]
                    send[z, move * 9 + rest] = scratch[step % 2, pl.ds(start + 8 - core * 8, 8), :]


def weigh_first(ids, mine, q_in, keep, send, own, scratch):
    for turn in range(4):
        own[(ids[0] + turn) & 3] = mine[turn, 128:256, :]
    weight_blocks(q_in, own[...].reshape(512, 128), keep, send, scratch, ids[2])


def weigh_second(
    ids, mine, before, after, other, matched, own, pick, pick_back, local, spread, lanes, sources,
    keep, send, q_hidden, scratch,
):
    @pl.loop(0, 4, unroll=2)
    def _(turn):
        at = (ids[0] + turn) & 3
        views = around(ids, mine, before, after, other, turn)
        found = dot(matched[at, :, :32], lanes[:, :768]).astype(BF)
        rows = [views[0][0:128, :]]
        rows += [view[device % 2 * 64 : device % 2 * 64 + 64, :] for device, view in enumerate(views[1:])]
        fill(q_hidden, at * 2, found, jnp.concatenate(rows, 0), pick[...], local[...], spread[...])

    weight_blocks(q_hidden, own[...].reshape(512, 128), keep, send, scratch, ids[2])


def apply_second(
    ids, mine, before, after, other, matched, q_hidden, weights, pick, pick_back, local, spread, lanes, sources,
    reduced, q_back,
):
    @pl.loop(0, 4, unroll=2)
    def _(turn):
        at = (ids[0] + turn) & 3
        views = around(ids, mine, before, after, other, turn)
        found = dot(matched[at, :, :32], lanes[:, 768:]).astype(BF)
        rows = jnp.concatenate([view[128:256, :] for view in views], 0)
        fill(q_back, at * 2, found, rows, pick_back[...], local[...], spread[...])

    forward = convolve(q_hidden, weights.at[1])
    backward = convolve_back(q_back, weights.at[0])
    for at in range(4):
        turn = (at - ids[1]) & 3
        reduced[turn, 0:128, :] = forward[at * 128 : (at + 1) * 128]
        reduced[turn, 128:256, :] = backward[at * 128 : (at + 1) * 128]


def call(kernel, outs, scratch, *args):
    smem = pl.BlockSpec(memory_space=pltpu.SMEM)
    vmem = pl.BlockSpec(memory_space=pltpu.VMEM)
    return pl.pallas_call(
        kernel,
        out_shape=outs,
        in_specs=[smem if value.dtype == jnp.int32 else vmem for value in args],
        out_specs=[vmem] * len(outs),
        scratch_shapes=scratch,
        compiler_params=pltpu.CompilerParams(vmem_limit_bytes=52 * 2**20),
    )(*args)


def turn_over(value, target):
    places = [(a, b) for a in range(4) for b in range(4)]
    moved = {place: tuple(v % 4 for v in target(*place)) for place in places}
    still = [place for place in places if moved[place] == place]
    for at, place in enumerate(still):
        moved[place] = still[(at + 1) % len(still)]
    came = lax.ppermute(value, ("x", "chan"), [(p[0] * 4 + p[1], q[0] * 4 + q[1]) for p, q in moved.items()])
    return (value, came) if still else (came, came)


def settled(value, came):
    return came if value is came else jnp.where(lax.axis_index("x") == lax.axis_index("chan"), value, came)


def spread_out(mine):
    before = lax.ppermute(mine, "z", [(i, (i + 1) % 8) for i in range(8)])
    after = lax.ppermute(mine, "z", [(i, (i - 1) % 8) for i in range(8)])
    cross = jnp.where(lax.axis_index("core") == 1, before, after)
    other = lax.ppermute(jnp.stack([mine, cross]), "core", [(0, 1), (1, 0)])
    return before, after, other


def on_device(features, mask, rulebook, weight_first, weight_second, cotangent):
    shape = jax.ShapeDtypeStruct
    x = lax.axis_index("x")
    core = lax.axis_index("core")
    here = lax.axis_index(SPACE)
    chan = lax.axis_index("chan")
    z = lax.axis_index("z")
    ids = jnp.stack([x, chan, core, (z == 0).astype(jnp.int32), (z == 7).astype(jnp.int32)]).astype(jnp.int32)

    shards = jnp.stack([weight_first, settled(*turn_over(weight_second, lambda a, b: (b, a)))])
    blocks = jnp.transpose(lax.all_gather(shards, ("z", "core"), axis=1, tiled=True), (0, 2, 1, 3))

    active = mask.astype(F32)[:, None]
    masked = (features.astype(F32) * active).astype(BF)
    grad_second = (cotangent.astype(F32) * active).astype(BF)

    padded = jnp.pad(rulebook.T, ((0, 5), (0, 0)), constant_values=-1)
    lane = np.arange(128)
    back_lane = np.where((lane >= 12) & (lane < 32), lane - 12, 0)
    read_by = np.where(lane < 12, lane // 6, back_lane % 2)
    reading = jnp.where(jnp.asarray(read_by == 0)[None], padded[:, 0:1], padded[:, 1:2])
    sources = np.array([0, 1, -2, -3, 2, 5])

    relative = jnp.where(reading >= 0, reading - here * 2, -(2**20))

    def lane_match(offsets, valid):
        target = np.where(valid, offsets, 2**20).astype(np.int32)
        return (relative == jnp.asarray(target)[None]).astype(BF)

    def back_match(position):
        valid = (lane >= 12) & (lane < 32) & (back_lane // 2 % 5 == position)
        step = 0 if position == 0 else STEPS[position - 1]
        return lane_match(2 * step + back_lane // 10, valid)

    compact = lane_match(sources[lane % 6], lane < 12)
    for position in range(5):
        compact = compact + back_match(position)
    packed = jnp.concatenate([masked[:64], grad_second, compact, masked[64:]], 0)
    turned = jnp.stack(
        [
            settled(*turn_over(packed, lambda a, b: (b, a - r)))
            for r in range(4)
        ]
    )
    consts = tables()
    columns = shape((8, 9, 96, 128), BF)
    q_in, q_back, own, matched = call(
        gather_first,
        [columns, columns, shape((4, 128, 128), BF), shape((4, 32, 128), BF)],
        [],
        ids,
        turned,
        *spread_out(turned),
        *consts,
    )
    (partial,) = call(apply_first, [shape((4, 256, 128), F32)], [], ids, q_in, q_back, blocks)
    summed = partial[0]
    for r in range(1, 4):
        summed = summed + lax.ppermute(partial[r], "x", [(a, (a + r) % 4) for a in range(4)])
    first_act = active * summed[0:128]
    hidden_grad = summed[128:256]
    sigmoid_first = jax.nn.sigmoid(first_act)
    hidden = (first_act * sigmoid_first).astype(BF)
    grad_first = (
        active * hidden_grad * sigmoid_first * (1.0 + first_act * (1.0 - sigmoid_first))
    ).astype(BF)

    packed = jnp.concatenate([hidden, grad_first], 0)
    along = jnp.stack(
        [packed] + [lax.ppermute(packed, "x", [(a, (a - r) % 4) for a in range(4)]) for r in range(1, 4)]
    )
    pieces = shape((8, 27, 8, 128), F32)
    pair = pltpu.VMEM((2, 384, 128), F32)
    keep1, send1 = call(weigh_first, [pieces, pieces], [pltpu.VMEM((4, 128, 128), BF), pair], ids, along, q_in)

    def both_cores(keep, send):
        return keep + lax.ppermute(send, "core", [(0, 1), (1, 0)])

    first_mine = both_cores(keep1, send1)
    first_sum = lax.psum_scatter(first_mine, "z", scatter_dimension=0, tiled=True).reshape(27, 8, 128)
    before, after, other, _ = lax.optimization_barrier((*spread_out(along), first_mine))
    keep2, send2, q_hidden = call(
        weigh_second,
        [pieces, pieces, columns],
        [pair],
        ids,
        along,
        before,
        after,
        other,
        matched,
        own,
        *consts,
    )
    second_mine = both_cores(keep2, send2).astype(BF).reshape(8, 216, 128)
    q_hidden, second_mine = lax.optimization_barrier((q_hidden, second_mine))
    moved = lax.all_to_all(second_mine, "z", 0, 0, tiled=True)
    (reduced,) = call(
        apply_second,
        [shape((4, 256, 128), F32)],
        [pltpu.VMEM((8, 9, 96, 128), BF)],
        ids,
        along,
        before,
        after,
        other,
        matched,
        q_hidden,
        blocks,
        *consts,
    )
    parts = [turn_over(reduced[r], lambda a, b: (b + r, a)) for r in range(4)]
    second_sum = jnp.sum(moved.astype(F32), axis=0).reshape(27, 8, 128)
    turned_sum = settled(*turn_over(second_sum, lambda a, b: (b, a)))
    *came, _ = lax.optimization_barrier((*(part[1] for part in parts), second_sum))
    second_sum = turned_sum
    total = settled(parts[0][0], came[0]) + came[1] + came[2] + came[3]
    output = (active * total[0:128]).astype(BF)
    features_grad = (active * total[128:256]).astype(BF)

    return (
        output,
        features_grad,
        jnp.transpose(first_sum, (1, 0, 2)),
        jnp.transpose(second_sum, (1, 0, 2)),
    )


def solution(mesh):
    split = Mesh(mesh.devices.reshape(4, 8, 2, 4), ("x", "z", "core", "chan"))
    placed = (
        P(SPACE, "chan"),
        P(SPACE),
        P(SPACE, None),
        P(SPACE, None, "chan"),
        P(SPACE, None, "chan"),
        P(SPACE, "chan"),
    )
    return jax.shard_map(
        on_device,
        mesh=split,
        in_specs=placed,
        out_specs=(
            P(SPACE, "chan"),
            P(SPACE, "chan"),
            P(SPACE, None, "chan"),
            P(SPACE, None, "chan"),
        ),
        check_vma=False,
    )
```

```python
import jax
import jax.numpy as jnp
import numpy as np
from jax import lax
from jax.experimental import pallas as pl
from jax.experimental.pallas import tpu as pltpu
from jax.sharding import Mesh
from jax.sharding import PartitionSpec as P

STEPS = (1, 2, -1, -2)
SPACE = ("x", "z", "core")
CELLS = 224
BF = jnp.bfloat16
F32 = jnp.float32


def tables():
    pick = np.zeros((CELLS, 32), np.float32)
    pick_back = np.zeros((CELLS, 32), np.float32)
    local = np.zeros((CELLS, 128), np.float32)
    for row in range(216):
        cell = (row // 36, row // 6 % 6, row % 6)
        side = [(v == 5) - (v == 0) for v in cell]
        at = [(v - 1) % 4 for v in cell]
        pick[row, 9 * (side[0] + 1) + 3 * (side[1] + 1) + side[2] + 1] = 1
        pick_back[row, 9 * (1 - side[0]) + 3 * (1 - side[1]) + 1 - side[2]] = 1
        voxel = at[0] * 16 + at[1] * 4 + at[2]
        local[row, voxel] = 1
        local[row, 64 + voxel] = 1
    spread = np.zeros((9, 6, 4, 4, CELLS), np.float32)
    for move in range(9):
        for i in range(6):
            for j in range(4):
                for k in range(4):
                    spread[move, i, j, k, i * 36 + (j + move // 3) * 6 + k + move % 3] = 1
    lanes = np.zeros((32, 2048), np.float32)
    for brick in range(2):
        for column in range(384):
            lanes[brick * 6 + column // 64, brick * 384 + column] = 1
        for column in range(640):
            lanes[12 + brick * 10 + column // 64, 768 + brick * 640 + column] = 1
    lane = np.arange(128)
    device = np.where((lane >= 12) & (lane < 32), (lane - 12) % 10 // 2, 0)
    sources = np.zeros((16, 128), np.float32)
    sources[device, lane] = 1
    as_bf = lambda value: jnp.asarray(value, BF)
    return (
        as_bf(pick),
        as_bf(pick_back),
        jnp.asarray(local),
        as_bf(spread.reshape(864, CELLS)),
        as_bf(lanes),
        as_bf(sources),
    )


def dot(a, b):
    return jnp.dot(a, b, preferred_element_type=F32)


def fill(out, base, matches, rows, pick, local, spread):
    count = rows.shape[0]
    chosen = dot(pick, matches)
    select = (chosen * jnp.concatenate([local] * (count // 64), axis=1)).astype(BF)
    found = dot(jnp.concatenate([select[:, :count], select[:, count:]], axis=0), rows).astype(BF)
    wide = dot(spread, jnp.concatenate([found[:CELLS], found[CELLS:]], axis=1)).astype(BF)
    for brick in range(2):
        out[base + brick] = wide[:, brick * 128 : (brick + 1) * 128].reshape(9, 96, 128)


def block(ref, offset):
    start = offset // 9 * 16
    return ref[:, offset % 9, start : start + 64, :].reshape(512, 128)


def convolve(ref, weight):
    total = None
    for offset in range(27):
        part = dot(block(ref, offset), weight[offset])
        total = part if total is None else total + part
    return total


def convolve_back(ref, weight):
    total = None
    for offset in range(27):
        part = lax.dot_general(
            block(ref, 26 - offset), weight[offset], (((1,), (1,)), ((), ())), preferred_element_type=F32
        )
        total = part if total is None else total + part
    return total


def around(ids, own, before, after, other, turn):
    return (
        own.at[turn],
        other.at[1 - ids[2], (turn - ids[3] * (1 - ids[2])) & 3],
        before.at[(turn - ids[3]) & 3],
        other.at[ids[2], (turn + ids[4] * ids[2]) & 3],
        after.at[(turn + ids[4]) & 3],
    )


def gather_first(
    ids, mine, before, after, other, pick, pick_back, local, spread, lanes, sources, q_in, q_back, own, matched
):
    @pl.loop(0, 4, unroll=2)
    def _(turn):
        at = (ids[1] + turn) & 3
        views = around(ids, mine, before, after, other, turn)
        compact = None
        for device, view in enumerate(views):
            part = view[192:224, :] * sources[device : device + 1, :]
            compact = part if compact is None else compact + part
        matched[at] = compact
        own[at] = views[0][64:192, :]
        found = dot(compact[:, :32], lanes[...]).astype(BF)
        rows = [views[0][0:64, :], views[0][224:288, :]]
        rows += [view[device % 2 * 224 : device % 2 * 224 + 64, :] for device, view in enumerate(views[1:])]
        fill(q_in, at * 2, found[:, :768], jnp.concatenate(rows, 0), pick[...], local[...], spread[...])
        rows = jnp.concatenate([view[64:192, :] for view in views], 0)
        fill(q_back, at * 2, found[:, 768:], rows, pick_back[...], local[...], spread[...])


def apply_first(ids, q_in, q_back, weights, out):
    forward = convolve(q_in, weights.at[0])
    backward = convolve_back(q_back, weights.at[1])
    for at in range(4):
        turn = (at - ids[0]) & 3
        out[turn, 0:128, :] = forward[at * 128 : (at + 1) * 128]
        out[turn, 128:256, :] = backward[at * 128 : (at + 1) * 128]


def weight_blocks(ref, gradient, keep, send, scratch, core):
    turned = gradient.T

    @pl.loop(0, 3)
    def _(side):
        for step in range(3):
            rest = side * 3 + step
            columns = [ref[:, rest, move * 16 : move * 16 + 64, :].reshape(512, 128) for move in range(3)]
            found = dot(turned, jnp.concatenate(columns, 1))
            for move in range(3):
                scratch[step % 2, move * 128 : (move + 1) * 128] = found[:, move * 128 : (move + 1) * 128].T
                for z in range(8):
                    start = move * 128 + z * 16
                    keep[z, move * 9 + rest] = scratch[step % 2, pl.ds(start + core * 8, 8), :]
                    send[z, move * 9 + rest] = scratch[step % 2, pl.ds(start + 8 - core * 8, 8), :]


def weigh_first(ids, mine, q_in, keep, send, own, scratch):
    for turn in range(4):
        own[(ids[0] + turn) & 3] = mine[turn, 128:256, :]
    weight_blocks(q_in, own[...].reshape(512, 128), keep, send, scratch, ids[2])


def weigh_second(
    ids, mine, before, after, other, matched, own, pick, pick_back, local, spread, lanes, sources,
    keep, send, q_hidden, scratch,
):
    @pl.loop(0, 4, unroll=4)
    def _(turn):
        at = (ids[0] + turn) & 3
        views = around(ids, mine, before, after, other, turn)
        found = dot(matched[at, :, :32], lanes[:, :768]).astype(BF)
        rows = [views[0][0:128, :]]
        rows += [view[device % 2 * 64 : device % 2 * 64 + 64, :] for device, view in enumerate(views[1:])]
        fill(q_hidden, at * 2, found, jnp.concatenate(rows, 0), pick[...], local[...], spread[...])

    weight_blocks(q_hidden, own[...].reshape(512, 128), keep, send, scratch, ids[2])


def apply_second(
    ids, mine, before, after, other, matched, q_hidden, weights, pick, pick_back, local, spread, lanes, sources,
    reduced, q_back,
):
    @pl.loop(0, 4, unroll=2)
    def _(turn):
        at = (ids[0] + turn) & 3
        views = around(ids, mine, before, after, other, turn)
        found = dot(matched[at, :, :32], lanes[:, 768:]).astype(BF)
        rows = jnp.concatenate([view[128:256, :] for view in views], 0)
        fill(q_back, at * 2, found, rows, pick_back[...], local[...], spread[...])

    forward = convolve(q_hidden, weights.at[1])
    backward = convolve_back(q_back, weights.at[0])
    for at in range(4):
        turn = (at - ids[1]) & 3
        reduced[turn, 0:128, :] = forward[at * 128 : (at + 1) * 128]
        reduced[turn, 128:256, :] = backward[at * 128 : (at + 1) * 128]


def call(kernel, outs, scratch, *args):
    smem = pl.BlockSpec(memory_space=pltpu.SMEM)
    vmem = pl.BlockSpec(memory_space=pltpu.VMEM)
    return pl.pallas_call(
        kernel,
        out_shape=outs,
        in_specs=[smem if value.dtype == jnp.int32 else vmem for value in args],
        out_specs=[vmem] * len(outs),
        scratch_shapes=scratch,
        compiler_params=pltpu.CompilerParams(vmem_limit_bytes=52 * 2**20),
    )(*args)


def turn_over(value, target):
    places = [(a, b) for a in range(4) for b in range(4)]
    moved = {place: tuple(v % 4 for v in target(*place)) for place in places}
    still = [place for place in places if moved[place] == place]
    for at, place in enumerate(still):
        moved[place] = still[(at + 1) % len(still)]
    came = lax.ppermute(value, ("x", "chan"), [(p[0] * 4 + p[1], q[0] * 4 + q[1]) for p, q in moved.items()])
    return (value, came) if still else (came, came)


def settled(value, came):
    return came if value is came else jnp.where(lax.axis_index("x") == lax.axis_index("chan"), value, came)


def spread_out(mine):
    before = lax.ppermute(mine, "z", [(i, (i + 1) % 8) for i in range(8)])
    after = lax.ppermute(mine, "z", [(i, (i - 1) % 8) for i in range(8)])
    cross = jnp.where(lax.axis_index("core") == 1, before, after)
    other = lax.ppermute(jnp.stack([mine, cross]), "core", [(0, 1), (1, 0)])
    return before, after, other


def on_device(features, mask, rulebook, weight_first, weight_second, cotangent):
    shape = jax.ShapeDtypeStruct
    x = lax.axis_index("x")
    core = lax.axis_index("core")
    here = lax.axis_index(SPACE)
    chan = lax.axis_index("chan")
    z = lax.axis_index("z")
    ids = jnp.stack([x, chan, core, (z == 0).astype(jnp.int32), (z == 7).astype(jnp.int32)]).astype(jnp.int32)

    shards = jnp.stack([weight_first, settled(*turn_over(weight_second, lambda a, b: (b, a)))])
    blocks = jnp.transpose(lax.all_gather(shards, ("z", "core"), axis=1, tiled=True), (0, 2, 1, 3))

    active = mask.astype(F32)[:, None]
    masked = (features.astype(F32) * active).astype(BF)
    grad_second = (cotangent.astype(F32) * active).astype(BF)

    padded = jnp.pad(rulebook.T, ((0, 5), (0, 0)), constant_values=-1)
    lane = np.arange(128)
    back_lane = np.where((lane >= 12) & (lane < 32), lane - 12, 0)
    read_by = np.where(lane < 12, lane // 6, back_lane % 2)
    reading = jnp.where(jnp.asarray(read_by == 0)[None], padded[:, 0:1], padded[:, 1:2])
    sources = np.array([0, 1, -2, -3, 2, 5])

    relative = jnp.where(reading >= 0, reading - here * 2, -(2**20))

    def lane_match(offsets, valid):
        target = np.where(valid, offsets, 2**20).astype(np.int32)
        return (relative == jnp.asarray(target)[None]).astype(BF)

    def back_match(position):
        valid = (lane >= 12) & (lane < 32) & (back_lane // 2 % 5 == position)
        step = 0 if position == 0 else STEPS[position - 1]
        return lane_match(2 * step + back_lane // 10, valid)

    compact = lane_match(sources[lane % 6], lane < 12)
    for position in range(5):
        compact = compact + back_match(position)
    packed = jnp.concatenate([masked[:64], grad_second, compact, masked[64:]], 0)
    turned = jnp.stack(
        [
            settled(*turn_over(packed, lambda a, b: (b, a - r)))
            for r in range(4)
        ]
    )
    consts = tables()
    columns = shape((8, 9, 96, 128), BF)
    q_in, q_back, own, matched = call(
        gather_first,
        [columns, columns, shape((4, 128, 128), BF), shape((4, 32, 128), BF)],
        [],
        ids,
        turned,
        *spread_out(turned),
        *consts,
    )
    (partial,) = call(apply_first, [shape((4, 256, 128), F32)], [], ids, q_in, q_back, blocks)
    summed = partial[0]
    for r in range(1, 4):
        summed = summed + lax.ppermute(partial[r], "x", [(a, (a + r) % 4) for a in range(4)])
    first_act = active * summed[0:128]
    hidden_grad = summed[128:256]
    sigmoid_first = jax.nn.sigmoid(first_act)
    hidden = (first_act * sigmoid_first).astype(BF)
    grad_first = (
        active * hidden_grad * sigmoid_first * (1.0 + first_act * (1.0 - sigmoid_first))
    ).astype(BF)

    packed = jnp.concatenate([hidden, grad_first], 0)
    along = jnp.stack(
        [packed] + [lax.ppermute(packed, "x", [(a, (a - r) % 4) for a in range(4)]) for r in range(1, 4)]
    )
    pieces = shape((8, 27, 8, 128), F32)
    pair = pltpu.VMEM((2, 384, 128), F32)
    keep1, send1 = call(weigh_first, [pieces, pieces], [pltpu.VMEM((4, 128, 128), BF), pair], ids, along, q_in)

    def both_cores(keep, send):
        return keep + lax.ppermute(send, "core", [(0, 1), (1, 0)])

    first_mine = both_cores(keep1, send1)
    first_sum = lax.psum_scatter(first_mine, "z", scatter_dimension=0, tiled=True).reshape(27, 8, 128)
    before, after, other, _ = lax.optimization_barrier((*spread_out(along), first_mine))
    keep2, send2, q_hidden = call(
        weigh_second,
        [pieces, pieces, columns],
        [pair],
        ids,
        along,
        before,
        after,
        other,
        matched,
        own,
        *consts,
    )
    second_mine = both_cores(keep2, send2).astype(BF).reshape(8, 216, 128)
    q_hidden, second_mine = lax.optimization_barrier((q_hidden, second_mine))
    moved = lax.all_to_all(second_mine, "z", 0, 0, tiled=True)
    (reduced,) = call(
        apply_second,
        [shape((4, 256, 128), F32)],
        [pltpu.VMEM((8, 9, 96, 128), BF)],
        ids,
        along,
        before,
        after,
        other,
        matched,
        q_hidden,
        blocks,
        *consts,
    )
    parts = [turn_over(reduced[r], lambda a, b: (b + r, a)) for r in range(4)]
    second_sum = jnp.sum(moved.astype(F32), axis=0).reshape(27, 8, 128)
    turned_sum = settled(*turn_over(second_sum, lambda a, b: (b, a)))
    *came, _ = lax.optimization_barrier((*(part[1] for part in parts), second_sum))
    second_sum = turned_sum
    total = settled(parts[0][0], came[0]) + came[1] + came[2] + came[3]
    output = (active * total[0:128]).astype(BF)
    features_grad = (active * total[128:256]).astype(BF)

    return (
        output,
        features_grad,
        jnp.transpose(first_sum, (1, 0, 2)),
        jnp.transpose(second_sum, (1, 0, 2)),
    )


def solution(mesh):
    split = Mesh(mesh.devices.reshape(4, 8, 2, 4), ("x", "z", "core", "chan"))
    placed = (
        P(SPACE, "chan"),
        P(SPACE),
        P(SPACE, None),
        P(SPACE, None, "chan"),
        P(SPACE, None, "chan"),
        P(SPACE, "chan"),
    )
    return jax.shard_map(
        on_device,
        mesh=split,
        in_specs=placed,
        out_specs=(
            P(SPACE, "chan"),
            P(SPACE, "chan"),
            P(SPACE, None, "chan"),
            P(SPACE, None, "chan"),
        ),
        check_vma=False,
    )
```
